32 devices in a mesh: fsdp: 8 (over y, x, core), dp: 4 (over z).
Axes of the slice: x: 2, y: 2, z: 4, core: 2. Of those that a mesh axis runs over, the one named last changes fastest.
Arguments:
- tokens: bfloat16 [8, 1024, 1024], P('fsdp', 'dp'), may hold values from -6 to 6
- segment: int32 [8, 1024], P('fsdp', 'dp'), may hold values from 0 to 5, never falling along the last dimension, each value on 1 to 512 neighbouring positions
- grad_out: bfloat16 [8, 1024, 1024], P('fsdp', 'dp'), may hold values from -6 to 6
- w_query: bfloat16 [1024, 1024], P(('fsdp', 'dp')), may hold values from -0.1875 to 0.1875
- w_key: bfloat16 [1024, 1024], P(('fsdp', 'dp')), may hold values from -0.1875 to 0.1875
- w_value: bfloat16 [1024, 1024], P(('fsdp', 'dp')), may hold values from -0.1875 to 0.1875
- w_out: bfloat16 [1024, 1024], P(('fsdp', 'dp')), may hold values from -0.75 to 0.75
- b_query: bfloat16 [1024], P(('fsdp', 'dp')), may hold values from -3 to 3
- b_value: bfloat16 [1024], P(('fsdp', 'dp')), may hold values from -3 to 3
- b_out: bfloat16 [1024], P(('fsdp', 'dp')), may hold values from -2 to 2
- norm1_gain: bfloat16 [1024], P(('fsdp', 'dp')), may hold values from 0.5 to 1.5
- norm1_bias: bfloat16 [1024], P(('fsdp', 'dp')), may hold values from -2 to 2
- w_in: bfloat16 [1024, 4096], P(('fsdp', 'dp')), may hold values from -0.1875 to 0.1875
- b_in: bfloat16 [4096], P(('fsdp', 'dp')), may hold values from -3 to 3
- w_back: bfloat16 [4096, 1024], P(('fsdp', 'dp')), may hold values from -0.09375 to 0.09375
- b_back: bfloat16 [1024], P(('fsdp', 'dp')), may hold values from -2 to 2
- norm2_gain: bfloat16 [1024], P(('fsdp', 'dp')), may hold values from 0.5 to 1.5
- norm2_bias: bfloat16 [1024], P(('fsdp', 'dp')), may hold values from -2 to 2
Outputs:
- layer_out: bfloat16 [8, 1024, 1024], P('fsdp', 'dp')
- grad_tokens: float32 [8, 1024, 1024], P('fsdp', 'dp')
- grad_w_query: float32 [1024, 1024], P(('fsdp', 'dp'))
- grad_w_key: float32 [1024, 1024], P(('fsdp', 'dp'))
- grad_w_value: float32 [1024, 1024], P(('fsdp', 'dp'))
- grad_w_out: float32 [1024, 1024], P(('fsdp', 'dp'))
- grad_b_query: float32 [1024], P(('fsdp', 'dp'))
- grad_b_value: float32 [1024], P(('fsdp', 'dp'))
- grad_b_out: float32 [1024], P(('fsdp', 'dp'))
- grad_norm1_gain: float32 [1024], P(('fsdp', 'dp'))
- grad_norm1_bias: float32 [1024], P(('fsdp', 'dp'))
- grad_w_in: float32 [1024, 4096], P(('fsdp', 'dp'))
- grad_b_in: float32 [4096], P(('fsdp', 'dp'))
- grad_w_back: float32 [4096, 1024], P(('fsdp', 'dp'))
- grad_b_back: float32 [1024], P(('fsdp', 'dp'))
- grad_norm2_gain: float32 [1024], P(('fsdp', 'dp'))
- grad_norm2_bias: float32 [1024], P(('fsdp', 'dp'))
The draws below stay inside these ranges and needn't reach their ends.
Inputs may be any that keep to these rules, and one draw needn't show every extreme that they name: segment numbers never fall along a sequence; a segment has at most 512 positions.
All inputs are finite; a program needn't handle non-finite values.
Results may differ from the reference program's by a relative error of at most 0.014.
Values may be sent and summed in bfloat16 or wider, within the bound.
No kernel may reach another device: no remote copies, remote signals or barrier semaphores. Data moves between devices by JAX's collectives and lax.ppermute only.
A program may use at most 192 MiB of HBM per device.

```python
import math
import jax
import jax.numpy as jnp
import numpy as np
from jax import lax

D = 1024
HEAD_DIM = 64
FF = 4096
SEQ_LEN = 1024
SEGS = 6
MOST_SEG = 512
SEQS = 8


def strengthened(drawn, key, source, target, blocks, factor):
    owner, partner = [(jnp.arange(drawn.shape[axis_at]) // (drawn.shape[axis_at] // blocks)).reshape([-1 if axis == axis_at else 1 for axis in range(drawn.ndim)]) for axis_at in (source, target)]
    chosen = jax.random.permutation(key, blocks)[partner]
    strong = (owner == chosen) | (owner == (partner + blocks // 2) % blocks)
    return jnp.where(strong, factor * drawn, drawn)


def shard_levels(rng, dims, shards, least, largest):
    factor_of, own = 1.0, jax.random.fold_in(rng, 6)
    for position, shards_of in shards:
        steps = jnp.exp(jax.random.uniform(jax.random.fold_in(own, position), (shards_of,), jnp.float32, least / len(shards), largest / len(shards)))
        factor_of = factor_of * jnp.repeat(steps, dims[position] // shards_of).reshape([-1 if axis == position else 1 for axis in range(len(dims))])
    return factor_of


def profile(amount, total, most, skew):
    weights = [(1 << 20) // math.isqrt(standing ** skew) + 1 for standing in range(2, amount + 1)]
    surplus, holding = total - most - (amount - 1), [1] * (amount - 1)
    while surplus > 0:
        movable = [i for i in range(amount - 1) if holding[i] < most]
        whole, left = sum([weights[i] for i in movable]), surplus
        for i in movable:
            extra = min(most - holding[i], max(1, left * weights[i] // whole), surplus)
            holding[i] = holding[i] + extra
            surplus = surplus - extra
    return np.array([most] + holding)


def ragged(rng, count, total, most, skew):
    if count == 2:
        one = jax.random.randint(rng, (), max(1, total - most), min(most, total - 1) + 1)
        return jnp.stack([one, total - one])
    sizes = jnp.asarray(profile(count, total, most, skew), jnp.int32)
    couples = (count - 1) // 2
    giver, taker = sizes[1:1 + 2 * couples:2], sizes[2:2 + 2 * couples:2]
    room = jnp.minimum(giver - 1, most - taker)
    passed = jax.random.randint(jax.random.fold_in(rng, 1), (couples,), 0, 1 << 20) % (room + 1)
    sizes = sizes.at[1:1 + 2 * couples:2].set(giver - passed).at[2:2 + 2 * couples:2].set(taker + passed)
    return sizes[jax.random.permutation(jax.random.fold_in(rng, 2), count)]


def bell_draw(rng, extent, deviation, most, split=(), dtype=jnp.bfloat16):
    level = shard_levels(rng, extent, split, -0.22, 0.18) if split else 1.0
    entries = jax.random.normal(rng, extent, jnp.float32) * deviation * level
    return jnp.minimum(jnp.maximum(entries, -most), most).astype(dtype)


def noise_with(own_key, shape, spread, reach, pieces, heavy, kind=jnp.bfloat16):
    entries = spread * jax.random.normal(own_key, shape, jnp.float32)
    if pieces:
        entries = entries * shard_levels(own_key, shape, pieces, -0.22, 0.18)
    return jnp.clip(strengthened(entries, jax.random.fold_in(own_key, 3), *heavy), -reach, reach).astype(kind)


def setup_inputs(seed: int = 0) -> dict:
    arg_keys = jax.random.split(jax.random.key(seed), 19)
    return {
        "tokens": bell_draw(arg_keys[0], (SEQS, SEQ_LEN, D), 1.0, 6.0, ((0, 8), (1, 4))),
        "segment": jax.vmap(lambda own: jnp.searchsorted(jnp.cumsum(ragged(own, SEGS, SEQ_LEN, MOST_SEG, 2)), jnp.arange(SEQ_LEN), side="right"))(jax.random.split(arg_keys[1], SEQS)).reshape((SEQS, SEQ_LEN)).astype(jnp.int32),
        "grad_out": noise_with(arg_keys[2], (SEQS, SEQ_LEN, D), 1.0, 6.0, ((0, 8), (1, 4)), (0, 2, 8, 2.0)),
        "w_query": bell_draw(arg_keys[3], (D, D), D ** -0.5, 0.1875, ((0, 32),)),
        "w_key": bell_draw(arg_keys[4], (D, D), D ** -0.5, 0.1875, ((0, 32),)),
        "w_value": bell_draw(arg_keys[5], (D, D), D ** -0.5, 0.1875, ((0, 32),)),
        "w_out": bell_draw(arg_keys[6], (D, D), (D // 16) ** -0.5, 0.75, ((0, 32),)),
        "b_query": bell_draw(arg_keys[7], (D,), 0.5, 3.0, ((0, 32),)),
        "b_value": bell_draw(arg_keys[8], (D,), 0.5, 3.0, ((0, 32),)),
        "b_out": bell_draw(arg_keys[9], (D,), 0.3, 2.0, ((0, 32),)),
        "norm1_gain": jnp.clip(1.0 + 0.1 * jax.random.normal(arg_keys[10], (D,), jnp.float32), 0.5, 1.5).astype(jnp.bfloat16),
        "norm1_bias": bell_draw(arg_keys[11], (D,), 0.3, 2.0, ((0, 32),)),
        "w_in": bell_draw(arg_keys[12], (D, FF), D ** -0.5, 0.1875, ((0, 32),)),
        "b_in": bell_draw(arg_keys[13], (FF,), 0.5, 3.0, ((0, 32),)),
        "w_back": bell_draw(arg_keys[14], (FF, D), FF ** -0.5, 0.09375, ((0, 32),)),
        "b_back": bell_draw(arg_keys[15], (D,), 0.3, 2.0, ((0, 32),)),
        "norm2_gain": jnp.clip(1.0 + 0.1 * jax.random.normal(arg_keys[16], (D,), jnp.float32), 0.5, 1.5).astype(jnp.bfloat16),
        "norm2_bias": bell_draw(arg_keys[17], (D,), 0.3, 2.0, ((0, 32),)),
    }


@jax.custom_vjp
def low(v):
    return lax.optimization_barrier(v.astype(jnp.bfloat16)).astype(jnp.float32)

@jax.custom_vjp
def low_back(v):
    return v

def low_keep(v):
    return (low(v), None)

def low_pass(kept, grad):
    return (grad,)

def back_keep(v):
    return (v, None)

def back_low(kept, grad):
    return (low(grad),)
low.defvjp(low_keep, low_pass)
low_back.defvjp(back_keep, back_low)
precise = lax.Precision.HIGHEST
norm_eps = 1e-05

def product(left, right):
    return jnp.dot(left, right, precision=precise)

def normalize(rows_in, gain, shift):
    mean_rows = lax.optimization_barrier(jnp.mean(rows_in, axis=-1, keepdims=True))
    centered = rows_in - mean_rows
    variance = lax.optimization_barrier(jnp.mean(centered * centered, axis=-1, keepdims=True))
    return centered * lax.rsqrt(variance + norm_eps) * gain + shift

def layer_block(tokens_in, segment_in, weight_list):
    q_weight, k_weight, v_weight, o_weight, q_bias, v_bias, o_bias, gain_one, shift_one, in_weight, in_bias, out_weight, out_bias, gain_two, shift_two = weight_list
    seq_count, seq_length, model_width = tokens_in.shape
    head_count = model_width // HEAD_DIM
    flat_tokens = tokens_in.reshape(seq_count * seq_length, model_width)
    query = low(low_back(product(flat_tokens, q_weight) + q_bias))
    key_rows = low(low_back(product(flat_tokens, k_weight)))
    value_rows = low(low_back(product(flat_tokens, v_weight) + v_bias))
    head_shape = (seq_count, seq_length, head_count, HEAD_DIM)
    scores = jnp.einsum('sqhe,skhe->shqk', query.reshape(head_shape), key_rows.reshape(head_shape), precision=precise) * HEAD_DIM ** (-0.5)
    scores = low_back(scores)
    same_segment = segment_in[:, None, :, None] == segment_in[:, None, None, :]
    scores = jnp.where(same_segment, scores, -1000000000.0)
    soft_weights = low(jax.nn.softmax(scores, axis=-1))
    mixed = jnp.einsum('shqk,skhe->sqhe', soft_weights, value_rows.reshape(head_shape), precision=precise)
    mixed = low(low_back(mixed.reshape(seq_count * seq_length, model_width)))
    branch = low_back(product(mixed, o_weight) + o_bias)
    hidden = normalize(flat_tokens + branch, gain_one, shift_one)
    pre_act = low_back(product(low(hidden), in_weight) + in_bias)
    activated = low(jax.nn.gelu(pre_act, approximate=False))
    mlp_out = low_back(product(activated, out_weight) + out_bias)
    result = normalize(hidden + mlp_out, gain_two, shift_two)
    return result.reshape(seq_count, seq_length, model_width)

def layer_all(tokens_in, segment_in, weight_list):
    seq_count = tokens_in.shape[0]
    block_seqs = 2 if seq_count % 2 == 0 else 1
    blocks = tokens_in.reshape((seq_count // block_seqs, block_seqs) + tokens_in.shape[1:])
    seg_blocks = segment_in.reshape((seq_count // block_seqs, block_seqs) + segment_in.shape[1:])

    def one_block(block_in):
        return layer_block(block_in[0], block_in[1], weight_list)
    outputs = lax.map(jax.checkpoint(one_block), (blocks, seg_blocks))
    return outputs.reshape(tokens_in.shape)

def reference(tokens, segment, grad_out, w_query, w_key, w_value, w_out, b_query, b_value, b_out, norm1_gain, norm1_bias, w_in, b_in, w_back, b_back, norm2_gain, norm2_bias):
    weight_list = tuple((weight_arg.astype(jnp.float32) for weight_arg in (w_query, w_key, w_value, w_out, b_query, b_value, b_out, norm1_gain, norm1_bias, w_in, b_in, w_back, b_back, norm2_gain, norm2_bias)))

    def run_layer(tokens_in, *weight_args):
        return layer_all(tokens_in, segment, weight_args)
    result, pull_back = jax.vjp(run_layer, tokens.astype(jnp.float32), *weight_list)
    grads = pull_back(grad_out.astype(jnp.float32))
    return (result.astype(jnp.bfloat16), grads[0], grads[1], grads[2], grads[3], grads[4], grads[5], grads[6], grads[7], grads[8], grads[9], grads[10], grads[11], grads[12], grads[13], grads[14], grads[15])
```

```python
from functools import partial

import jax
import jax.numpy as jnp
from jax import lax
from jax.experimental import pallas as pl
from jax.experimental.pallas import tpu as pltpu
from jax.sharding import PartitionSpec as P

HEAD_DIM = 64
PAIR = 2 * HEAD_DIM
AXES = ("fsdp", "dp")
NORM_EPS = 1e-05
NEG_FILL = -1000000000.0
F32 = jnp.float32
BF16 = jnp.bfloat16


def matmul(left, right):
    return jnp.dot(left, right, preferred_element_type=F32)


def matmul_t(left, right):
    return lax.dot_general(left, right, (((1,), (1,)), ((), ())), preferred_element_type=F32)


def outer_sum(left, right):
    return lax.dot_general(left, right, (((0,), (0,)), ((), ())), preferred_element_type=F32)


def col_sums(values):
    return jnp.sum(values.astype(F32), axis=0)


def normalize(rows_in, gain, shift):
    mean_rows = jnp.mean(rows_in, axis=-1, keepdims=True)
    centered = rows_in - mean_rows
    inverse = lax.rsqrt(jnp.mean(centered * centered, axis=-1, keepdims=True) + NORM_EPS)
    normed = centered * inverse
    return normed * gain + shift, normed, inverse


def normalize_back(grad_rows, normed, inverse, gain):
    scaled = grad_rows * gain
    return inverse * (
        scaled
        - jnp.mean(scaled, axis=-1, keepdims=True)
        - normed * jnp.mean(scaled * normed, axis=-1, keepdims=True)
    )


def head_lanes(rows, head):
    lane = lax.broadcasted_iota(jnp.int32, (rows, PAIR), 1)
    return (lane // HEAD_DIM) == head


def pair_scores(query, key, head, same):
    own = jnp.where(head_lanes(query.shape[0], head), query, jnp.zeros_like(query))
    raw = matmul_t(own, key) * (HEAD_DIM ** -0.5)
    return jnp.where(same, raw, NEG_FILL)


def attend_kernel(seg_q, seg_k, query, key, value, mixed, log_total):
    same = seg_q[...] == seg_k[...]
    rows = query.shape[0]
    outs, logs = [], []
    for head in range(2):
        scores = pair_scores(query[...], key[...], head, same)
        top = jnp.max(scores, axis=-1, keepdims=True)
        expo = jnp.exp(scores - top)
        total = jnp.sum(expo, axis=-1, keepdims=True)
        soft = (expo / total).astype(BF16)
        outs.append(matmul(soft, value[...]))
        logs.append(top + jnp.log(total))
    first = head_lanes(rows, 0)
    mixed[...] = jnp.where(first, outs[0], outs[1]).astype(BF16)
    log_total[...] = jnp.where(first, logs[0], logs[1])


def attend_back_kernel(
    seg_q, seg_k, query, key, value, log_total, grad_mixed, grad_query, grad_key, grad_value
):
    same = seg_q[...] == seg_k[...]
    rows = query.shape[0]
    dq, dk, dv = [], [], []
    for head in range(2):
        scores = pair_scores(query[...], key[...], head, same)
        probs = jnp.exp(scores - log_total[:, head * HEAD_DIM : head * HEAD_DIM + 1])
        grad_own = jnp.where(
            head_lanes(rows, head), grad_mixed[...], jnp.zeros_like(grad_mixed[...])
        )
        grad_probs = matmul_t(grad_own, value[...])
        row_sum = jnp.sum(grad_probs * probs, axis=-1, keepdims=True)
        grad_scores = (probs * (grad_probs - row_sum)).astype(BF16)
        dv.append(outer_sum(probs.astype(BF16), grad_mixed[...]))
        dq.append(matmul(grad_scores, key[...]))
        dk.append(outer_sum(grad_scores, query[...]))
    first = head_lanes(rows, 0)
    first_k = head_lanes(key.shape[0], 0)
    scale = HEAD_DIM ** -0.5
    grad_query[...] = (jnp.where(first, dq[0], dq[1]) * scale).astype(BF16)
    grad_key[...] = (jnp.where(first_k, dk[0], dk[1]) * scale).astype(BF16)
    grad_value[...] = jnp.where(first_k, dv[0], dv[1]).astype(BF16)


def attend(seg_q, seg_k, query, key, value):
    rows, width = query.shape
    full = key.shape[0]
    narrow = pl.BlockSpec((rows, PAIR), lambda p: (0, p))
    wide = pl.BlockSpec((full, PAIR), lambda p: (0, p))
    return pl.pallas_call(
        attend_kernel,
        grid=(width // PAIR,),
        in_specs=[
            pl.BlockSpec((rows, 1), lambda p: (0, 0)),
            pl.BlockSpec((1, full), lambda p: (0, 0)),
            narrow,
            wide,
            wide,
        ],
        out_specs=[narrow, narrow],
        out_shape=[
            jax.ShapeDtypeStruct((rows, width), BF16),
            jax.ShapeDtypeStruct((rows, width), F32),
        ],
        name="attend",
    )(seg_q, seg_k, query, key, value)


def attend_back(seg_q, seg_k, query, key, value, log_total, grad_mixed):
    rows, width = query.shape
    full = key.shape[0]
    narrow = pl.BlockSpec((rows, PAIR), lambda p: (0, p))
    wide = pl.BlockSpec((full, PAIR), lambda p: (0, p))
    return pl.pallas_call(
        attend_back_kernel,
        grid=(width // PAIR,),
        in_specs=[
            pl.BlockSpec((rows, 1), lambda p: (0, 0)),
            pl.BlockSpec((1, full), lambda p: (0, 0)),
            narrow,
            wide,
            wide,
            narrow,
            narrow,
        ],
        out_specs=[narrow, wide, wide],
        out_shape=[
            jax.ShapeDtypeStruct((rows, width), BF16),
            jax.ShapeDtypeStruct((full, width), BF16),
            jax.ShapeDtypeStruct((full, width), BF16),
        ],
        name="attend_back",
    )(seg_q, seg_k, query, key, value, log_total, grad_mixed)


def split_cols(block, width):
    rows, cols = block.shape
    parts = cols // width
    return block.reshape(rows, parts, width).transpose(1, 0, 2).reshape(rows * parts, width)


def gather_rows(block):
    count, width = block.shape
    whole = lax.all_gather(block, AXES, axis=0, tiled=True)
    return whole.reshape(-1, count, width)


def join_cols(stack, parts):
    devices, rows, width = stack.shape
    own = rows // parts
    return (
        stack.reshape(devices, parts, own, width)
        .transpose(0, 2, 1, 3)
        .reshape(devices * own, parts * width)
    )


def join_rows(stack):
    return stack.reshape(-1, stack.shape[-1])


def body(
    tokens,
    segment,
    grad_out,
    w_query,
    w_key,
    w_value,
    w_out,
    b_query,
    b_value,
    b_out,
    norm1_gain,
    norm1_bias,
    w_in,
    b_in,
    w_back,
    b_back,
    norm2_gain,
    norm2_bias,
):
    groups, rows, width = tokens.shape
    own = w_query.shape[0]
    ffn = w_in.shape[1]
    in_parts = ffn // width
    own_ffn = w_back.shape[0]
    vectors = (b_query, b_value, b_out, norm1_gain, norm1_bias, b_back, norm2_gain, norm2_bias)
    count = len(vectors)

    flat = tokens.reshape(rows, width)
    wide_tokens = flat.astype(F32)
    small = jnp.concatenate(vectors + (b_in,))
    small_len = small.shape[0]
    small_rows = jnp.zeros((8, width), BF16).at[0, :small_len].set(small)

    tokens_all = lax.all_gather(flat, "dp", axis=0, tiled=True)
    seg_low = segment.astype(BF16)
    seg_all = lax.all_gather(seg_low, "dp", axis=1, tiled=True)
    seg_q = segment.reshape(rows, 1).astype(F32)
    seg_k = seg_all.astype(F32)

    attn = gather_rows(jnp.concatenate([w_query, w_key, w_value, w_out, small_rows]))
    q_weight, k_weight, v_weight, o_weight = (
        join_rows(attn[:, i * own : (i + 1) * own]) for i in range(4)
    )
    small_all = attn[:, 4 * own, :small_len].astype(F32)
    per = small_all[:, : count * own].reshape(-1, count, own).transpose(1, 0, 2).reshape(count, -1)
    q_bias, v_bias, o_bias, gain_one, shift_one, out_bias, gain_two, shift_two = (
        per[i] for i in range(count)
    )
    in_bias = small_all[:, count * own :].reshape(-1)

    mlp = gather_rows(jnp.concatenate([split_cols(w_in, width), w_back]))
    in_weight = join_cols(mlp[:, : own * in_parts], in_parts)
    out_weight = join_rows(mlp[:, own * in_parts :])

    query = (matmul(flat, q_weight) + q_bias).astype(BF16)
    key = matmul(tokens_all, k_weight).astype(BF16)
    value = (matmul(tokens_all, v_weight) + v_bias).astype(BF16)
    mixed, log_total = attend(seg_q, seg_k, query, key, value)

    branch = matmul(mixed, o_weight) + o_bias
    hidden, normed_one, inverse_one = normalize(wide_tokens + branch, gain_one, shift_one)
    hidden_low = hidden.astype(BF16)
    pre_act = matmul(hidden_low, in_weight) + in_bias
    activated = jax.nn.gelu(pre_act, approximate=False).astype(BF16)
    mlp_out = matmul(activated, out_weight) + out_bias
    result, normed_two, inverse_two = normalize(hidden + mlp_out, gain_two, shift_two)
    layer_out = result.astype(BF16).reshape(tokens.shape)

    grad_top = grad_out.reshape(rows, width).astype(F32)
    grad_res_two = normalize_back(grad_top, normed_two, inverse_two, gain_two)
    grad_gain_two = jnp.sum(grad_top * normed_two, axis=0)
    grad_shift_two = jnp.sum(grad_top, axis=0)
    grad_mlp = grad_res_two.astype(BF16)
    grad_out_bias = col_sums(grad_mlp)
    grad_out_weight = outer_sum(activated, grad_mlp).astype(BF16)
    grad_act = matmul_t(grad_mlp, out_weight)
    gelu_pull = jax.vjp(partial(jax.nn.gelu, approximate=False), pre_act)[1]
    grad_pre = gelu_pull(grad_act)[0].astype(BF16)
    grad_in_bias = col_sums(grad_pre)
    grad_in_weight = outer_sum(hidden_low, grad_pre).astype(BF16)
    grad_hidden = matmul_t(grad_pre, in_weight) + grad_res_two

    devices = attn.shape[0]

    def by_device(grad):
        return grad.reshape(devices, -1, width)

    in_blocks = (
        grad_in_weight.reshape(devices, own, in_parts, width)
        .transpose(0, 2, 1, 3)
        .reshape(devices, own * in_parts, width)
    )
    mlp_blocks = jnp.concatenate([in_blocks, by_device(grad_out_weight)], axis=1)
    mlp_sum = lax.psum_scatter(join_rows(mlp_blocks), AXES, scatter_dimension=0, tiled=True)

    grad_res_one = normalize_back(grad_hidden, normed_one, inverse_one, gain_one)
    grad_gain_one = jnp.sum(grad_hidden * normed_one, axis=0)
    grad_shift_one = jnp.sum(grad_hidden, axis=0)
    grad_branch = grad_res_one.astype(BF16)
    grad_o_bias = col_sums(grad_branch)
    grad_o_weight = outer_sum(mixed, grad_branch).astype(BF16)
    grad_mixed = matmul_t(grad_branch, o_weight).astype(BF16)
    grad_query, grad_key, grad_value = attend_back(
        seg_q, seg_k, query, key, value, log_total, grad_mixed
    )
    grad_q_bias = col_sums(grad_query)
    grad_v_bias = col_sums(grad_value)
    grad_q_weight = outer_sum(flat, grad_query).astype(BF16)
    grad_k_weight = outer_sum(tokens_all, grad_key).astype(BF16)
    grad_v_weight = outer_sum(tokens_all, grad_value).astype(BF16)
    spread = (matmul_t(grad_key, k_weight) + matmul_t(grad_value, v_weight)).astype(BF16)
    spread_own = lax.psum_scatter(spread, "dp", scatter_dimension=0, tiled=True).astype(F32)
    grad_input = grad_res_one + matmul_t(grad_query, q_weight) + spread_own

    grad_vectors = jnp.stack(
        [
            grad_q_bias,
            grad_v_bias,
            grad_o_bias,
            grad_gain_one,
            grad_shift_one,
            grad_out_bias,
            grad_gain_two,
            grad_shift_two,
        ]
    )
    grad_small = jnp.concatenate(
        [
            grad_vectors.reshape(count, devices, own).transpose(1, 0, 2).reshape(devices, -1),
            grad_in_bias.reshape(devices, own_ffn),
        ],
        axis=1,
    ).astype(BF16)
    small_block = jnp.zeros((devices, 8, width), BF16).at[:, 0, :small_len].set(grad_small)
    attn_blocks = jnp.concatenate(
        [
            by_device(grad_q_weight),
            by_device(grad_k_weight),
            by_device(grad_v_weight),
            by_device(grad_o_weight),
            small_block,
        ],
        axis=1,
    )
    attn_sum = lax.psum_scatter(join_rows(attn_blocks), AXES, scatter_dimension=0, tiled=True)
    attn_sum = attn_sum.astype(F32)
    small_sum = attn_sum[4 * own, :small_len]
    vec = [small_sum[i * own : (i + 1) * own] for i in range(count)]
    grad_b_in = small_sum[count * own :]
    mlp_sum = mlp_sum.astype(F32)
    grad_w_in = (
        mlp_sum[: own * in_parts]
        .reshape(in_parts, own, width)
        .transpose(1, 0, 2)
        .reshape(own, ffn)
    )
    return (
        layer_out,
        grad_input.reshape(tokens.shape),
        attn_sum[:own],
        attn_sum[own : 2 * own],
        attn_sum[2 * own : 3 * own],
        attn_sum[3 * own : 4 * own],
        vec[0],
        vec[1],
        vec[2],
        vec[3],
        vec[4],
        grad_w_in,
        grad_b_in,
        mlp_sum[own * in_parts :],
        vec[5],
        vec[6],
        vec[7],
    )


def solution(mesh):
    act = P("fsdp", "dp", None)
    mat = P(AXES, None)
    vec = P(AXES)
    return jax.shard_map(
        body,
        mesh=mesh,
        in_specs=(act, P("fsdp", "dp"), act, mat, mat, mat, mat)
        + (vec,) * 5
        + (mat, vec, mat, vec, vec, vec),
        out_specs=(act, act, mat, mat, mat, mat) + (vec,) * 5 + (mat, vec, mat, vec, vec, vec),
        check_vma=False,
    )
```

```python
from functools import partial

import jax
import jax.numpy as jnp
from jax import lax
from jax.experimental import pallas as pl
from jax.experimental.pallas import tpu as pltpu
from jax.sharding import PartitionSpec as P

HEAD_DIM = 64
PAIR = 2 * HEAD_DIM
AXES = ("fsdp", "dp")
NORM_EPS = 1e-05
NEG_FILL = -1000000000.0
F32 = jnp.float32
BF16 = jnp.bfloat16


def matmul(left, right):
    return jnp.dot(left, right, preferred_element_type=F32)


def matmul_t(left, right):
    return lax.dot_general(left, right, (((1,), (1,)), ((), ())), preferred_element_type=F32)


def outer_sum(left, right):
    return lax.dot_general(left, right, (((0,), (0,)), ((), ())), preferred_element_type=F32)


def col_sums(values):
    return jnp.sum(values.astype(F32), axis=0)


def normalize(rows_in, gain, shift):
    mean_rows = jnp.mean(rows_in, axis=-1, keepdims=True)
    centered = rows_in - mean_rows
    inverse = lax.rsqrt(jnp.mean(centered * centered, axis=-1, keepdims=True) + NORM_EPS)
    normed = centered * inverse
    return normed * gain + shift, normed, inverse


def normalize_back(grad_rows, normed, inverse, gain):
    scaled = grad_rows * gain
    return inverse * (
        scaled
        - jnp.mean(scaled, axis=-1, keepdims=True)
        - normed * jnp.mean(scaled * normed, axis=-1, keepdims=True)
    )


def head_lanes(rows, head):
    lane = lax.broadcasted_iota(jnp.int32, (rows, PAIR), 1)
    return (lane // HEAD_DIM) == head


def pair_scores(query, key, head, same):
    own = jnp.where(head_lanes(query.shape[0], head), query, jnp.zeros_like(query))
    raw = matmul_t(own, key) * (HEAD_DIM ** -0.5)
    return jnp.where(same, raw, NEG_FILL)


def attend_kernel(seg_q, seg_k, query, key, value, mixed, log_total):
    same = seg_q[...] == seg_k[...]
    rows = query.shape[0]
    outs, logs = [], []
    for head in range(2):
        scores = pair_scores(query[...], key[...], head, same)
        top = jnp.max(scores, axis=-1, keepdims=True)
        expo = jnp.exp(scores - top)
        total = jnp.sum(expo, axis=-1, keepdims=True)
        soft = (expo / total).astype(BF16)
        outs.append(matmul(soft, value[...]))
        logs.append(top + jnp.log(total))
    first = head_lanes(rows, 0)
    mixed[...] = jnp.where(first, outs[0], outs[1]).astype(BF16)
    log_total[...] = jnp.where(first, logs[0], logs[1])


def attend_back_kernel(
    seg_q, seg_k, query, key, value, log_total, grad_mixed, grad_query, grad_key, grad_value
):
    same = seg_q[...] == seg_k[...]
    rows = query.shape[0]
    dq, dk, dv = [], [], []
    for head in range(2):
        scores = pair_scores(query[...], key[...], head, same)
        probs = jnp.exp(scores - log_total[:, head * HEAD_DIM : head * HEAD_DIM + 1])
        grad_own = jnp.where(
            head_lanes(rows, head), grad_mixed[...], jnp.zeros_like(grad_mixed[...])
        )
        grad_probs = matmul_t(grad_own, value[...])
        row_sum = jnp.sum(grad_probs * probs, axis=-1, keepdims=True)
        grad_scores = (probs * (grad_probs - row_sum)).astype(BF16)
        dv.append(outer_sum(probs.astype(BF16), grad_mixed[...]))
        dq.append(matmul(grad_scores, key[...]))
        dk.append(outer_sum(grad_scores, query[...]))
    first = head_lanes(rows, 0)
    first_k = head_lanes(key.shape[0], 0)
    scale = HEAD_DIM ** -0.5
    grad_query[...] = (jnp.where(first, dq[0], dq[1]) * scale).astype(BF16)
    grad_key[...] = (jnp.where(first_k, dk[0], dk[1]) * scale).astype(BF16)
    grad_value[...] = jnp.where(first_k, dv[0], dv[1]).astype(BF16)


def attend(seg_q, seg_k, query, key, value):
    rows, width = query.shape
    full = key.shape[0]
    narrow = pl.BlockSpec((rows, PAIR), lambda p: (0, p))
    wide = pl.BlockSpec((full, PAIR), lambda p: (0, p))
    return pl.pallas_call(
        attend_kernel,
        grid=(width // PAIR,),
        in_specs=[
            pl.BlockSpec((rows, 1), lambda p: (0, 0)),
            pl.BlockSpec((1, full), lambda p: (0, 0)),
            narrow,
            wide,
            wide,
        ],
        out_specs=[narrow, narrow],
        out_shape=[
            jax.ShapeDtypeStruct((rows, width), BF16),
            jax.ShapeDtypeStruct((rows, width), F32),
        ],
        name="attend",
    )(seg_q, seg_k, query, key, value)


def attend_back(seg_q, seg_k, query, key, value, log_total, grad_mixed):
    rows, width = query.shape
    full = key.shape[0]
    narrow = pl.BlockSpec((rows, PAIR), lambda p: (0, p))
    wide = pl.BlockSpec((full, PAIR), lambda p: (0, p))
    return pl.pallas_call(
        attend_back_kernel,
        grid=(width // PAIR,),
        in_specs=[
            pl.BlockSpec((rows, 1), lambda p: (0, 0)),
            pl.BlockSpec((1, full), lambda p: (0, 0)),
            narrow,
            wide,
            wide,
            narrow,
            narrow,
        ],
        out_specs=[narrow, wide, wide],
        out_shape=[
            jax.ShapeDtypeStruct((rows, width), BF16),
            jax.ShapeDtypeStruct((full, width), BF16),
            jax.ShapeDtypeStruct((full, width), BF16),
        ],
        name="attend_back",
    )(seg_q, seg_k, query, key, value, log_total, grad_mixed)


def coordinate(bit):
    return (lax.axis_index("fsdp") // bit) % 2


def hop(block, bit):
    count = lax.axis_size("fsdp")
    return lax.ppermute(block, "fsdp", [(i, i ^ bit) for i in range(count)])


def shift(block, step):
    count = lax.axis_size("dp")
    return lax.ppermute(block, "dp", [(i, (i + step) % count) for i in range(count)])


def chip_bits():
    bits = []
    bit = 2
    while bit < lax.axis_size("fsdp"):
        bits.append(bit)
        bit *= 2
    return bits


def after(block, earlier):
    return lax.optimization_barrier((block, earlier))[0]


def gather_line(block):
    count = lax.axis_size("dp")
    place = lax.axis_index("dp")
    whole = jnp.broadcast_to(block[None], (count,) + block.shape)
    for step in range(1, count):
        got = shift(block, step)
        whole = lax.dynamic_update_index_in_dim(whole, got, (place - step) % count, 0)
    return whole


def double(block, bit, held):
    got = hop(block, bit)
    low_side = coordinate(bit) == 0
    axis = sum(1 for other in held if other > bit)
    return jnp.stack(
        [jnp.where(low_side, block, got), jnp.where(low_side, got, block)], axis=axis
    )


def gather_chips(block, order):
    held = []
    for bit in order + [1]:
        block = double(block, bit, held)
        held.append(bit)
    return block.reshape(-1, block.shape[-1])


def gather_pair(lined, width):
    flat = lined.reshape(-1, lined.shape[-1])
    bits = chip_bits()
    return gather_chips(flat[:, :width], bits), gather_chips(flat[:, width:], bits[::-1])


def core_columns(left, which):
    count = lax.axis_size("fsdp")
    wide = left.shape[1] // count
    odd = which == 1
    return jnp.concatenate(
        [
            jnp.where(
                odd,
                left[:, (i + 1) * wide : (i + 2) * wide],
                left[:, i * wide : (i + 1) * wide],
            )
            for i in range(0, count, 2)
        ],
        axis=1,
    )


def reduce_chips(terms, order):
    core = coordinate(1)
    send = jnp.concatenate([outer_sum(other, right).astype(BF16) for _, other, right in terms], 1)
    got = hop(send, 1)
    keep = jnp.concatenate([outer_sum(mine, right) for mine, _, right in terms], 1)
    total = keep + got.astype(F32)
    bits = chip_bits()[::-1]
    width = total.shape[-1]
    total = total.astype(BF16).reshape((2,) * len(bits) + (-1, width))
    for bit in order:
        axis = bits.index(bit)
        bits = bits[:axis] + bits[axis + 1 :]
        mine = coordinate(bit)
        got = hop(lax.dynamic_index_in_dim(total, 1 - mine, axis, keepdims=False), bit)
        kept = lax.dynamic_index_in_dim(total, mine, axis, keepdims=False)
        total = (kept.astype(F32) + got.astype(F32)).astype(BF16)
    return total.reshape(-1, width)


def reduce_line(total):
    count = lax.axis_size("dp")
    place = lax.axis_index("dp")
    blocks = total.reshape(count, -1, total.shape[-1])
    own = lax.dynamic_index_in_dim(blocks, place, 0, keepdims=False).astype(F32)
    for step in range(1, count):
        sent = lax.dynamic_index_in_dim(blocks, (place + step) % count, 0, keepdims=False)
        own = own + shift(sent, step).astype(F32)
    return own


def reduce_pair(first, second):
    bits = chip_bits()[::-1]
    one = reduce_chips(first, bits)
    two = reduce_chips(second, bits[::-1])
    return reduce_line(jnp.concatenate([one, two], axis=1))


def both_cores(left):
    core = coordinate(1)
    return core_columns(left, core), core_columns(left, 1 - core)


def body(
    tokens,
    segment,
    grad_out,
    w_query,
    w_key,
    w_value,
    w_out,
    b_query,
    b_value,
    b_out,
    norm1_gain,
    norm1_bias,
    w_in,
    b_in,
    w_back,
    b_back,
    norm2_gain,
    norm2_bias,
):
    groups, rows, width = tokens.shape
    own = w_query.shape[0]
    ffn = w_in.shape[1]
    own_ffn = w_back.shape[0]
    half, half_ffn = width // 2, ffn // 2
    devices = lax.axis_size(AXES)
    vectors = (b_query, b_value, b_out, norm1_gain, norm1_bias, b_back, norm2_gain, norm2_bias)
    count = len(vectors)

    flat = tokens.reshape(rows, width)
    wide_tokens = flat.astype(F32)

    small = jnp.concatenate(vectors + (b_in, segment.reshape(rows).astype(BF16)))
    small_all = lax.all_gather(small, AXES, axis=0).astype(F32)
    small_len = count * own + own_ffn
    seg_rows = small_all[:, small_len:].reshape(lax.axis_size("fsdp"), -1)
    seg_k = lax.dynamic_index_in_dim(seg_rows, lax.axis_index("fsdp"), 0)
    seg_q = segment.reshape(rows, 1).astype(F32)
    per = small_all[:, : count * own].reshape(-1, count, own).transpose(1, 0, 2).reshape(count, -1)
    q_bias, v_bias, o_bias, gain_one, shift_one, out_bias, gain_two, shift_two = (
        per[i] for i in range(count)
    )
    in_bias = small_all[:, count * own : small_len].reshape(-1)

    attn_line = gather_line(jnp.concatenate([w_key, w_value, w_query, w_out], axis=1))
    kv_weight, qo_weight = gather_pair(attn_line, 2 * width)
    tokens_all = gather_line(after(flat, attn_line)).reshape(-1, width)
    in_line = gather_line(after(w_in, tokens_all))
    in_weights = gather_pair(in_line, half_ffn)
    out_line = gather_line(after(w_back, in_line))
    out_weights = gather_pair(out_line, half)

    q_weight, o_weight = qo_weight[:, :width], qo_weight[:, width:]
    query = (matmul(flat, q_weight) + q_bias).astype(BF16)
    key = matmul(tokens_all, kv_weight[:, :width]).astype(BF16)
    value = (matmul(tokens_all, kv_weight[:, width:]) + v_bias).astype(BF16)
    mixed, log_total = attend(seg_q, seg_k, query, key, value)

    branch = matmul(mixed, o_weight) + o_bias
    hidden, normed_one, inverse_one = normalize(wide_tokens + branch, gain_one, shift_one)
    hidden_low = hidden.astype(BF16)
    pre_act = [
        matmul(hidden_low, in_weights[i]) + in_bias[i * half_ffn : (i + 1) * half_ffn]
        for i in range(2)
    ]
    activated = jnp.concatenate(
        [jax.nn.gelu(part, approximate=False).astype(BF16) for part in pre_act], axis=1
    )
    mlp_out = jnp.concatenate([matmul(activated, part) for part in out_weights], axis=1) + out_bias
    result, normed_two, inverse_two = normalize(hidden + mlp_out, gain_two, shift_two)
    layer_out = result.astype(BF16).reshape(tokens.shape)

    grad_top = grad_out.reshape(rows, width).astype(F32)
    grad_res_two = normalize_back(grad_top, normed_two, inverse_two, gain_two)
    grad_gain_two = jnp.sum(grad_top * normed_two, axis=0)
    grad_shift_two = jnp.sum(grad_top, axis=0)
    grad_mlp = grad_res_two.astype(BF16)
    grad_out_bias = col_sums(grad_mlp)
    act_mine, act_other = both_cores(activated)
    back_sum = reduce_pair(
        [(act_mine, act_other, grad_mlp[:, :half])], [(act_mine, act_other, grad_mlp[:, half:])]
    )
    grad_act = matmul_t(grad_mlp[:, :half], out_weights[0]) + matmul_t(
        grad_mlp[:, half:], out_weights[1]
    )
    grad_pre = [
        jax.vjp(partial(jax.nn.gelu, approximate=False), pre_act[i])[1](
            grad_act[:, i * half_ffn : (i + 1) * half_ffn]
        )[0].astype(BF16)
        for i in range(2)
    ]
    grad_in_bias = jnp.concatenate([col_sums(part) for part in grad_pre])
    low_mine, low_other = both_cores(hidden_low)
    in_sum = reduce_pair([(low_mine, low_other, grad_pre[0])], [(low_mine, low_other, grad_pre[1])])
    grad_hidden = (
        matmul_t(grad_pre[0], in_weights[0]) + matmul_t(grad_pre[1], in_weights[1]) + grad_res_two
    )

    grad_res_one = normalize_back(grad_hidden, normed_one, inverse_one, gain_one)
    grad_gain_one = jnp.sum(grad_hidden * normed_one, axis=0)
    grad_shift_one = jnp.sum(grad_hidden, axis=0)
    grad_branch = grad_res_one.astype(BF16)
    grad_o_bias = col_sums(grad_branch)
    grad_mixed = matmul_t(grad_branch, o_weight).astype(BF16)
    grad_query, grad_key, grad_value = attend_back(
        seg_q, seg_k, query, key, value, log_total, grad_mixed
    )
    grad_q_bias = col_sums(grad_query)
    grad_v_bias = col_sums(grad_value)
    spread = (
        matmul_t(grad_key, kv_weight[:, :width]) + matmul_t(grad_value, kv_weight[:, width:])
    ).astype(BF16)
    spread_own = reduce_line(spread)
    all_mine, all_other = both_cores(tokens_all)
    flat_mine, flat_other = both_cores(flat)
    mixed_mine, mixed_other = both_cores(mixed)
    attn_sum = reduce_pair(
        [(all_mine, all_other, grad_key), (all_mine, all_other, grad_value)],
        [(flat_mine, flat_other, grad_query), (mixed_mine, mixed_other, grad_branch)],
    )
    grad_input = grad_res_one + matmul_t(grad_query, q_weight) + spread_own

    grad_vectors = jnp.stack(
        [
            grad_q_bias,
            grad_v_bias,
            grad_o_bias,
            grad_gain_one,
            grad_shift_one,
            grad_out_bias,
            grad_gain_two,
            grad_shift_two,
        ]
    )
    grad_small = jnp.concatenate(
        [
            grad_vectors.reshape(count, devices, own).transpose(1, 0, 2).reshape(devices, -1),
            grad_in_bias.reshape(devices, own_ffn),
        ],
        axis=1,
    )
    small_sum = lax.psum_scatter(grad_small, AXES, scatter_dimension=0, tiled=True)[0]
    vec = [small_sum[i * own : (i + 1) * own] for i in range(count)]
    return (
        layer_out,
        grad_input.reshape(tokens.shape),
        attn_sum[:, 2 * width : 3 * width],
        attn_sum[:, :width],
        attn_sum[:, width : 2 * width],
        attn_sum[:, 3 * width :],
        vec[0],
        vec[1],
        vec[2],
        vec[3],
        vec[4],
        in_sum,
        small_sum[count * own :],
        back_sum,
        vec[5],
        vec[6],
        vec[7],
    )


def solution(mesh):
    act = P("fsdp", "dp", None)
    mat = P(AXES, None)
    vec = P(AXES)
    return jax.shard_map(
        body,
        mesh=mesh,
        in_specs=(act, P("fsdp", "dp"), act, mat, mat, mat, mat)
        + (vec,) * 5
        + (mat, vec, mat, vec, vec, vec),
        out_specs=(act, act, mat, mat, mat, mat) + (vec,) * 5 + (mat, vec, mat, vec, vec, vec),
        check_vma=False,
    )
```

```python
from functools import partial

import jax
import jax.numpy as jnp
from jax import lax
from jax.experimental import pallas as pl
from jax.experimental.pallas import tpu as pltpu
from jax.sharding import PartitionSpec as P

HEAD_DIM = 64
PAIR = 2 * HEAD_DIM
AXES = ("fsdp", "dp")
NORM_EPS = 1e-05
NEG_FILL = -1000000000.0
F32 = jnp.float32
BF16 = jnp.bfloat16


def matmul(left, right):
    return jnp.dot(left, right, preferred_element_type=F32)


def matmul_t(left, right):
    return lax.dot_general(left, right, (((1,), (1,)), ((), ())), preferred_element_type=F32)


def outer_sum(left, right):
    return lax.dot_general(left, right, (((0,), (0,)), ((), ())), preferred_element_type=F32)


def col_sums(values):
    return jnp.sum(values.astype(F32), axis=0)


def normalize(rows_in, gain, shift):
    mean_rows = jnp.mean(rows_in, axis=-1, keepdims=True)
    centered = rows_in - mean_rows
    inverse = lax.rsqrt(jnp.mean(centered * centered, axis=-1, keepdims=True) + NORM_EPS)
    normed = centered * inverse
    return normed * gain + shift, normed, inverse


def normalize_back(grad_rows, normed, inverse, gain):
    scaled = grad_rows * gain
    return inverse * (
        scaled
        - jnp.mean(scaled, axis=-1, keepdims=True)
        - normed * jnp.mean(scaled * normed, axis=-1, keepdims=True)
    )


def head_lanes(rows, head):
    lane = lax.broadcasted_iota(jnp.int32, (rows, PAIR), 1)
    return (lane // HEAD_DIM) == head


def pair_scores(query, key, head, same):
    own = jnp.where(head_lanes(query.shape[0], head), query, jnp.zeros_like(query))
    raw = matmul_t(own, key) * (HEAD_DIM ** -0.5)
    return jnp.where(same, raw, NEG_FILL)


def attend_kernel(seg_q, seg_k, query, key, value, mixed, log_total):
    same = seg_q[...] == seg_k[...]
    rows = query.shape[0]
    outs, logs = [], []
    for head in range(2):
        scores = pair_scores(query[...], key[...], head, same)
        top = jnp.max(scores, axis=-1, keepdims=True)
        expo = jnp.exp(scores - top)
        total = jnp.sum(expo, axis=-1, keepdims=True)
        soft = (expo / total).astype(BF16)
        outs.append(matmul(soft, value[...]))
        logs.append(top + jnp.log(total))
    first = head_lanes(rows, 0)
    mixed[...] = jnp.where(first, outs[0], outs[1]).astype(BF16)
    log_total[...] = jnp.where(first, logs[0], logs[1])


def attend_back_kernel(
    seg_q, seg_k, query, key, value, log_total, grad_mixed, grad_query, grad_key, grad_value
):
    same = seg_q[...] == seg_k[...]
    rows = query.shape[0]
    dq, dk, dv = [], [], []
    for head in range(2):
        scores = pair_scores(query[...], key[...], head, same)
        probs = jnp.exp(scores - log_total[:, head * HEAD_DIM : head * HEAD_DIM + 1])
        grad_own = jnp.where(
            head_lanes(rows, head), grad_mixed[...], jnp.zeros_like(grad_mixed[...])
        )
        grad_probs = matmul_t(grad_own, value[...])
        row_sum = jnp.sum(grad_probs * probs, axis=-1, keepdims=True)
        grad_scores = (probs * (grad_probs - row_sum)).astype(BF16)
        dv.append(outer_sum(probs.astype(BF16), grad_mixed[...]))
        dq.append(matmul(grad_scores, key[...]))
        dk.append(outer_sum(grad_scores, query[...]))
    first = head_lanes(rows, 0)
    first_k = head_lanes(key.shape[0], 0)
    scale = HEAD_DIM ** -0.5
    grad_query[...] = (jnp.where(first, dq[0], dq[1]) * scale).astype(BF16)
    grad_key[...] = (jnp.where(first_k, dk[0], dk[1]) * scale).astype(BF16)
    grad_value[...] = jnp.where(first_k, dv[0], dv[1]).astype(BF16)


def attend(seg_q, seg_k, query, key, value):
    rows, width = query.shape
    full = key.shape[0]
    narrow = pl.BlockSpec((rows, PAIR), lambda p: (0, p))
    wide = pl.BlockSpec((full, PAIR), lambda p: (0, p))
    return pl.pallas_call(
        attend_kernel,
        grid=(width // PAIR,),
        in_specs=[
            pl.BlockSpec((rows, 1), lambda p: (0, 0)),
            pl.BlockSpec((1, full), lambda p: (0, 0)),
            narrow,
            wide,
            wide,
        ],
        out_specs=[narrow, narrow],
        out_shape=[
            jax.ShapeDtypeStruct((rows, width), BF16),
            jax.ShapeDtypeStruct((rows, width), F32),
        ],
        name="attend",
    )(seg_q, seg_k, query, key, value)


def attend_back(seg_q, seg_k, query, key, value, log_total, grad_mixed):
    rows, width = query.shape
    full = key.shape[0]
    narrow = pl.BlockSpec((rows, PAIR), lambda p: (0, p))
    wide = pl.BlockSpec((full, PAIR), lambda p: (0, p))
    return pl.pallas_call(
        attend_back_kernel,
        grid=(width // PAIR,),
        in_specs=[
            pl.BlockSpec((rows, 1), lambda p: (0, 0)),
            pl.BlockSpec((1, full), lambda p: (0, 0)),
            narrow,
            wide,
            wide,
            narrow,
            narrow,
        ],
        out_specs=[narrow, wide, wide],
        out_shape=[
            jax.ShapeDtypeStruct((rows, width), BF16),
            jax.ShapeDtypeStruct((full, width), BF16),
            jax.ShapeDtypeStruct((full, width), BF16),
        ],
        name="attend_back",
    )(seg_q, seg_k, query, key, value, log_total, grad_mixed)


def coordinate(bit):
    return (lax.axis_index("fsdp") // bit) % 2


def hop(block, bit):
    count = lax.axis_size("fsdp")
    return lax.ppermute(block, "fsdp", [(i, i ^ bit) for i in range(count)])


def shift(block, step):
    count = lax.axis_size("dp")
    return lax.ppermute(block, "dp", [(i, (i + step) % count) for i in range(count)])


def chip_bits():
    bits = []
    bit = 2
    while bit < lax.axis_size("fsdp"):
        bits.append(bit)
        bit *= 2
    return bits


def after(block, earlier):
    return lax.optimization_barrier((block, earlier))[0]


def pass_on(block, pairs):
    return lax.ppermute(block, "dp", pairs)


def gather_line(block):
    count = lax.axis_size("dp")
    place = lax.axis_index("dp")
    up, down = [block], [block]
    for step in range(1, count):
        pairs = [(i, i + 1) for i in range(step - 1, count - 1)]
        up.append(pass_on(up[-1], pairs))
        down.append(pass_on(down[-1], [(count - 1 - i, count - 1 - j) for i, j in pairs]))
    whole = jnp.broadcast_to(block[None], (count,) + block.shape)
    for step in range(1, count):
        got = jnp.where(place >= step, up[step], down[count - step])
        whole = lax.dynamic_update_index_in_dim(whole, got, (place - step) % count, 0)
    return whole


def double(block, bit, held):
    got = hop(block, bit)
    low_side = coordinate(bit) == 0
    axis = sum(1 for other in held if other > bit)
    return jnp.stack(
        [jnp.where(low_side, block, got), jnp.where(low_side, got, block)], axis=axis
    )


def gather_chips(block, order):
    held = []
    for bit in order + [1]:
        block = double(block, bit, held)
        held.append(bit)
    return block.reshape(-1, block.shape[-1])


def gather_pair(lined, width):
    flat = lined.reshape(-1, lined.shape[-1])
    bits = chip_bits()
    return gather_chips(flat[:, :width], bits), gather_chips(flat[:, width:], bits[::-1])


def core_columns(left, which):
    count = lax.axis_size("fsdp")
    wide = left.shape[1] // count
    odd = which == 1
    return jnp.concatenate(
        [
            jnp.where(
                odd,
                left[:, (i + 1) * wide : (i + 2) * wide],
                left[:, i * wide : (i + 1) * wide],
            )
            for i in range(0, count, 2)
        ],
        axis=1,
    )


def core_send(terms):
    return jnp.concatenate([outer_sum(other, right).astype(BF16) for _, other, right in terms], 1)


def core_total(terms, send):
    got = hop(send, 1)
    keep = jnp.concatenate([outer_sum(mine, right) for mine, _, right in terms], 1)
    return (keep + got.astype(F32)).astype(BF16)


def reduce_step(total, bits, bit):
    axis = bits.index(bit)
    mine = coordinate(bit)
    got = hop(lax.dynamic_index_in_dim(total, 1 - mine, axis, keepdims=False), bit)
    kept = lax.dynamic_index_in_dim(total, mine, axis, keepdims=False)
    return kept.astype(F32) + got.astype(F32)


def reduce_chips(total, order):
    bits = chip_bits()[::-1]
    width = total.shape[-1]
    total = total.reshape((2,) * len(bits) + (-1, width))
    for bit in order:
        total = reduce_step(total, bits, bit).astype(BF16)
        bits = [other for other in bits if other != bit]
    return total.reshape(-1, width)


def reduce_small(blocks):
    bits = chip_bits()[::-1] + [1]
    total = blocks.reshape((2,) * len(bits) + (-1,) + blocks.shape[1:])
    for bit in list(bits[::-1]):
        total = reduce_step(total, bits, bit)
        bits = [other for other in bits if other != bit]
    return reduce_line(total)


def reduce_line(total):
    count = lax.axis_size("dp")
    place = lax.axis_index("dp")
    blocks = total.reshape(count, -1, total.shape[-1])
    own = lax.dynamic_index_in_dim(blocks, place, 0, keepdims=False).astype(F32)
    for step in range(1, count):
        sent = lax.dynamic_index_in_dim(blocks, (place + step) % count, 0, keepdims=False)
        own = own + shift(sent, step).astype(F32)
    return own


def reduce_pair(first, second):
    bits = chip_bits()[::-1]
    one = reduce_chips(first, bits)
    two = reduce_chips(second, bits[::-1])
    return reduce_line(jnp.concatenate([one, two], axis=1))


def small_rows(values):
    count = -(-values.shape[0] // 1024) * 1024
    return jnp.zeros((count,), values.dtype).at[: values.shape[0]].set(values).reshape(-1, 128)


def both_cores(left):
    core = coordinate(1)
    return core_columns(left, core), core_columns(left, 1 - core)


def body(
    tokens,
    segment,
    grad_out,
    w_query,
    w_key,
    w_value,
    w_out,
    b_query,
    b_value,
    b_out,
    norm1_gain,
    norm1_bias,
    w_in,
    b_in,
    w_back,
    b_back,
    norm2_gain,
    norm2_bias,
):
    groups, rows, width = tokens.shape
    own = w_query.shape[0]
    ffn = w_in.shape[1]
    own_ffn = w_back.shape[0]
    half, half_ffn = width // 2, ffn // 2
    devices = lax.axis_size(AXES)
    vectors = (b_query, b_value, b_out, norm1_gain, norm1_bias, b_back, norm2_gain, norm2_bias)
    count = len(vectors)

    flat = tokens.reshape(rows, width)
    wide_tokens = flat.astype(F32)

    small_len = count * own + own_ffn
    small = jnp.concatenate(vectors + (b_in, segment.reshape(rows).astype(BF16)))
    small_line = gather_line(small_rows(small))
    place_rows = small_line.shape[1]
    seg_k = small_line.reshape(-1, place_rows * 128)[:, small_len : small_len + rows]
    seg_k = seg_k.reshape(1, -1).astype(F32)
    seg_q = segment.reshape(rows, 1).astype(F32)

    attn_line = gather_line(jnp.concatenate([w_key, w_value, w_query, w_out], axis=1))
    kv_weight, qo_weight = gather_pair(attn_line, 2 * width)
    small_all = gather_chips(after(small_line.reshape(-1, 128), attn_line), chip_bits())
    small_all = small_all.reshape(devices, -1)[:, :small_len].astype(F32)
    per = small_all[:, : count * own].reshape(-1, count, own).transpose(1, 0, 2).reshape(count, -1)
    q_bias, v_bias, o_bias, gain_one, shift_one, out_bias, gain_two, shift_two = (
        per[i] for i in range(count)
    )
    in_bias = small_all[:, count * own :].reshape(-1)

    in_line = gather_line(after(w_in, attn_line))
    in_weights = gather_pair(in_line, half_ffn)
    tokens_all = gather_line(after(flat, in_line)).reshape(-1, width)
    out_line = gather_line(after(w_back, tokens_all))
    out_weights = gather_pair(out_line, half)

    q_weight, o_weight = qo_weight[:, :width], qo_weight[:, width:]
    query = (matmul(flat, q_weight) + q_bias).astype(BF16)
    key = matmul(tokens_all, kv_weight[:, :width]).astype(BF16)
    value = (matmul(tokens_all, kv_weight[:, width:]) + v_bias).astype(BF16)
    mixed, log_total = attend(seg_q, seg_k, query, key, value)

    branch = matmul(mixed, o_weight) + o_bias
    hidden, normed_one, inverse_one = normalize(wide_tokens + branch, gain_one, shift_one)
    hidden_low = hidden.astype(BF16)
    pre_act = [
        matmul(hidden_low, in_weights[i]) + in_bias[i * half_ffn : (i + 1) * half_ffn]
        for i in range(2)
    ]
    activated = jnp.concatenate(
        [jax.nn.gelu(part, approximate=False).astype(BF16) for part in pre_act], axis=1
    )
    mlp_out = jnp.concatenate([matmul(activated, part) for part in out_weights], axis=1) + out_bias
    result, normed_two, inverse_two = normalize(hidden + mlp_out, gain_two, shift_two)
    layer_out = result.astype(BF16).reshape(tokens.shape)

    grad_top = grad_out.reshape(rows, width).astype(F32)
    grad_res_two = normalize_back(grad_top, normed_two, inverse_two, gain_two)
    grad_gain_two = jnp.sum(grad_top * normed_two, axis=0)
    grad_shift_two = jnp.sum(grad_top, axis=0)
    grad_mlp = grad_res_two.astype(BF16)
    grad_out_bias = col_sums(grad_mlp)
    act_mine, act_other = both_cores(activated)
    back_terms = [
        [(act_mine, act_other, grad_mlp[:, :half])],
        [(act_mine, act_other, grad_mlp[:, half:])],
    ]
    back_sends = [core_send(terms) for terms in back_terms]
    grad_mlp = after(grad_mlp, back_sends)
    grad_act = matmul_t(grad_mlp[:, :half], out_weights[0]) + matmul_t(
        grad_mlp[:, half:], out_weights[1]
    )
    grad_pre = [
        jax.vjp(partial(jax.nn.gelu, approximate=False), pre_act[i])[1](
            grad_act[:, i * half_ffn : (i + 1) * half_ffn]
        )[0].astype(BF16)
        for i in range(2)
    ]
    low_mine, low_other = both_cores(hidden_low)
    in_terms = [[(low_mine, low_other, part)] for part in grad_pre]
    in_sends = [core_send(terms) for terms in in_terms]
    back_totals = [core_total(terms, send) for terms, send in zip(back_terms, back_sends)]
    grad_pre = after(grad_pre, (in_sends, back_totals))
    grad_in_bias = jnp.concatenate([col_sums(part) for part in grad_pre])
    grad_hidden = (
        matmul_t(grad_pre[0], in_weights[0]) + matmul_t(grad_pre[1], in_weights[1]) + grad_res_two
    )

    grad_res_one = normalize_back(grad_hidden, normed_one, inverse_one, gain_one)
    grad_gain_one = jnp.sum(grad_hidden * normed_one, axis=0)
    grad_shift_one = jnp.sum(grad_hidden, axis=0)
    grad_branch = grad_res_one.astype(BF16)
    grad_o_bias = col_sums(grad_branch)
    grad_mixed = matmul_t(grad_branch, o_weight).astype(BF16)
    in_totals = [core_total(terms, send) for terms, send in zip(in_terms, in_sends)]
    back_sum = reduce_pair(*back_totals)
    in_sum = reduce_pair(*in_totals)
    grad_query, grad_key, grad_value = attend_back(
        seg_q, seg_k, query, key, value, log_total, after(grad_mixed, in_totals)
    )
    grad_q_bias = col_sums(grad_query)
    grad_v_bias = col_sums(grad_value)
    all_mine, all_other = both_cores(tokens_all)
    flat_mine, flat_other = both_cores(flat)
    mixed_mine, mixed_other = both_cores(mixed)
    attn_terms = [
        [(all_mine, all_other, grad_key), (all_mine, all_other, grad_value)],
        [(flat_mine, flat_other, grad_query), (mixed_mine, mixed_other, grad_branch)],
    ]
    attn_sends = [core_send(terms) for terms in attn_terms]
    grad_key, grad_value = after((grad_key, grad_value), attn_sends)
    spread = (
        matmul_t(grad_key, kv_weight[:, :width]) + matmul_t(grad_value, kv_weight[:, width:])
    ).astype(BF16)
    spread_own = reduce_line(spread)
    attn_totals = [core_total(terms, send) for terms, send in zip(attn_terms, attn_sends)]
    attn_sum = reduce_pair(*attn_totals)
    grad_input = grad_res_one + matmul_t(grad_query, q_weight) + spread_own

    grad_vectors = jnp.stack(
        [
            grad_q_bias,
            grad_v_bias,
            grad_o_bias,
            grad_gain_one,
            grad_shift_one,
            grad_out_bias,
            grad_gain_two,
            grad_shift_two,
        ]
    )
    grad_small = jnp.concatenate(
        [
            grad_vectors.reshape(count, devices, own).transpose(1, 0, 2).reshape(devices, -1),
            grad_in_bias.reshape(devices, own_ffn),
        ],
        axis=1,
    )
    small_sum = reduce_small(jax.vmap(small_rows)(grad_small)).reshape(-1)[:small_len]
    vec = [small_sum[i * own : (i + 1) * own] for i in range(count)]
    return (
        layer_out,
        grad_input.reshape(tokens.shape),
        attn_sum[:, 2 * width : 3 * width],
        attn_sum[:, :width],
        attn_sum[:, width : 2 * width],
        attn_sum[:, 3 * width :],
        vec[0],
        vec[1],
        vec[2],
        vec[3],
        vec[4],
        in_sum,
        small_sum[count * own :],
        back_sum,
        vec[5],
        vec[6],
        vec[7],
    )


def solution(mesh):
    act = P("fsdp", "dp", None)
    mat = P(AXES, None)
    vec = P(AXES)
    return jax.shard_map(
        body,
        mesh=mesh,
        in_specs=(act, P("fsdp", "dp"), act, mat, mat, mat, mat)
        + (vec,) * 5
        + (mat, vec, mat, vec, vec, vec),
        out_specs=(act, act, mat, mat, mat, mat) + (vec,) * 5 + (mat, vec, mat, vec, vec, vec),
        check_vma=False,
    )
```
